32 devices in a mesh: rep: 8 (over z, core), shard: 4 (over y, x).
Axes of the slice: x: 2, y: 2, z: 4, core: 2. Of those that a mesh axis runs over, the one named last changes fastest.
Arguments:
- hidden_in: float32 [4096, 1600], P(('rep', 'shard')), may hold values from -6 to 6
- segment_ids: int32 [8, 512], P('rep'), may hold values from 0 to 5, never falling along the last dimension, each value on 1 to 256 neighbouring positions
- span_order: int32 [8, 4], P('rep'), may hold values from 0 to 3, each once within a row
- qkv_weight: bfloat16 [1600, 4800], P('shard'), may hold values from -1 to 1
- out_weight: bfloat16 [1600, 1600], P('shard'), may hold values from -2 to 2
- up_weight: bfloat16 [1600, 6400], P('shard'), may hold values from -0.15625 to 0.15625
- down_weight: bfloat16 [6400, 1600], P('shard'), may hold values from -0.078125 to 0.078125
- vectors: bfloat16 [12, 1600], P(None, 'shard'), may hold values from -2 to 3
- cotangent: float32 [4096, 1600], P(('rep', 'shard')), may hold values from -6 to 6
Outputs:
- block_out: float32 [4096, 1600], P(('rep', 'shard'))
- input_grad: float32 [4096, 1600], P(('rep', 'shard'))
- qkv_grad: float32 [1600, 4800], P('shard')
- out_grad: float32 [1600, 1600], P('shard')
- up_grad: float32 [1600, 6400], P('shard')
- down_grad: float32 [6400, 1600], P('shard')
- vector_grad: float32 [12, 1600], P(None, 'shard')
The draws below stay inside these ranges and needn't reach their ends.
Inputs may be any that keep to these rules, and one draw needn't show every extreme that they name: `segment_ids`: numbers never fall along the positions of a sequence. `span_order`: each row is a permutation.
All inputs are finite; a program needn't handle non-finite values.
Results may differ from the reference program's by a relative error of at most 0.018.
Values may be sent and summed in bfloat16 or wider, within the bound.
No kernel may reach another device: no remote copies, remote signals or barrier semaphores. Data moves between devices by JAX's collectives and lax.ppermute only.
A program may use at most 384 MiB of HBM per device.

```python
import math
from functools import partial
import jax
import jax.numpy as jnp
import numpy as np
from jax import lax

D = 1600
HEADS = 25
FF = 6400
TOK_DEV = 128
DOCS = 6
LEN = 512
SEQS = 8
TOKENS = 4096
N_SHARD = 4


def draw_qkv_weight(key, part):
    drawn = jax.random.normal(key, (D, 3 * D), jnp.float32) * (1.0 / D ** 0.5)
    return jnp.clip(drawn, -1.0, 1.0).astype(jnp.bfloat16)


def draw_vectors(key, part):
    normal_draw = jax.random.normal(key, (12, D), jnp.float32)
    row_ids = jnp.arange(12)[:, None]
    gain_rows = jnp.exp(0.35 * jnp.clip(normal_draw, -3.0, 3.0))
    biases = 0.5 * jnp.clip(normal_draw, -4.0, 4.0)
    return jnp.where((row_ids == 0) | (row_ids == 5), gain_rows, biases).astype(jnp.bfloat16)


def block_scale(own_key, extent, cuts, smallest, largest):
    def one(position, shards_of):
        draws = jax.random.uniform(jax.random.fold_in(jax.random.fold_in(own_key, 6), position), (shards_of,), jnp.float32, smallest / len(cuts), largest / len(cuts))
        return jnp.repeat(jnp.exp(draws), extent[position] // shards_of).reshape((-1,) + (1,) * (len(extent) - position - 1))

    factor_of = one(*cuts[0])
    for cut in cuts[1:]:
        factor_of = factor_of * one(*cut)
    return factor_of


def profile(amount, total, limit, skew):
    weights = [(1 << 20) // math.isqrt(standing ** skew) + 1 for standing in range(2, amount + 1)]
    surplus, given = total - limit - (amount - 1), [1] * (amount - 1)
    while surplus > 0:
        free = [i for i in range(amount - 1) if given[i] < limit]
        pool, budget = sum([weights[i] for i in free]), surplus
        for i in free:
            addition = min(limit - given[i], max(1, budget * weights[i] // pool), surplus)
            given[i] = given[i] + addition
            surplus = surplus - addition
    return np.array([limit] + given)


def ragged(stream_key, amount, total, reach, skew):
    if amount == 2:
        one = jax.random.randint(stream_key, (), max(1, total - reach), min(reach, total - 1) + 1)
        return jnp.stack([one, total - one])
    tallies = jnp.asarray(profile(amount, total, reach, skew), jnp.int32)
    couples = (amount - 1) // 2
    giver, receiver = tallies[1:1 + 2 * couples:2], tallies[2:2 + 2 * couples:2]
    room = jnp.minimum(giver - 1, reach - receiver)
    shifted = jax.random.randint(jax.random.fold_in(stream_key, 1), (couples,), 0, 1 << 20) % (room + 1)
    tallies = tallies.at[1:1 + 2 * couples:2].set(giver - shifted).at[2:2 + 2 * couples:2].set(receiver + shifted)
    return tallies[jax.random.permutation(jax.random.fold_in(stream_key, 2), amount)]


def scatter_about(stream_key, shape, deviation, most, shards=(), kind=jnp.bfloat16):
    values = deviation * jax.random.normal(stream_key, shape, jnp.float32)
    if shards:
        values = values * block_scale(stream_key, shape, shards, -0.22, 0.18)
    return jnp.clip(values, -most, most).astype(kind)


def setup_inputs(seed: int = 0) -> dict:
    key_of = jax.random.split(jax.random.key(seed), 10)
    return {
        "hidden_in": scatter_about(key_of[0], (TOKENS, D), 1.0, 6.0, ((0, 32),), jnp.float32),
        "segment_ids": jax.vmap(lambda own: jnp.searchsorted(jnp.cumsum(ragged(own, DOCS, LEN, LEN // 2, 2)), jnp.arange(LEN), side="right"))(jax.random.split(key_of[1], SEQS)).reshape((SEQS, LEN)).astype(jnp.int32),
        "span_order": jax.vmap(lambda own: jax.random.permutation(own, N_SHARD))(jax.random.split(key_of[2], SEQS)).reshape((SEQS, N_SHARD)).astype(jnp.int32),
        "qkv_weight": draw_qkv_weight(jax.random.fold_in(key_of[9], 71), 0),
        "out_weight": scatter_about(key_of[4], (D, D), (max(D // 200, 1)) ** -0.5, 2.0, ((0, 4),)),
        "up_weight": scatter_about(key_of[5], (D, FF), D ** -0.5, 0.15625, ((0, 4),)),
        "down_weight": scatter_about(key_of[6], (FF, D), FF ** -0.5, 0.078125, ((0, 4),)),
        "vectors": draw_vectors(jax.random.fold_in(key_of[9], 71), 0),
        "cotangent": scatter_about(key_of[8], (TOKENS, D), 1.0, 6.0, ((0, 32),), jnp.float32),
    }


eps_norm = 1e-05
gelu_c = math.sqrt(2.0 / math.pi)

def product(left_side, right_side):
    return jnp.dot(left_side, right_side, preferred_element_type=jnp.float32)

def product_left(left_side, right_side):
    return lax.dot_general(left_side, right_side, (((0,), (0,)), ((), ())), preferred_element_type=jnp.float32)

def product_right(left_side, right_side):
    return lax.dot_general(left_side, right_side, (((1,), (1,)), ((), ())), preferred_element_type=jnp.float32)

def normalize(inputs):
    average = lax.optimization_barrier(jnp.mean(inputs, axis=1, keepdims=True))
    centred = inputs - average
    inverse = lax.rsqrt(lax.optimization_barrier(jnp.mean(centred * centred, axis=1, keepdims=True)) + eps_norm)
    return (centred * inverse, inverse)

def norm_back(upstream, normed, inverse, gain_row):
    scaled = upstream * gain_row
    return inverse * (scaled - lax.optimization_barrier(jnp.mean(scaled, axis=1, keepdims=True)) - normed * lax.optimization_barrier(jnp.mean(scaled * normed, axis=1, keepdims=True)))

def gelu_pair(preact):
    tangent = jnp.tanh(gelu_c * (preact + 0.044715 * preact * preact * preact))
    activated = 0.5 * preact * (1.0 + tangent)
    derivative = 0.5 * (1.0 + tangent) + 0.5 * preact * (1.0 - tangent * tangent) * gelu_c * (1.0 + 0.134145 * preact * preact)
    return (activated, derivative)

def split_heads(matrix):
    return matrix.reshape(matrix.shape[0], HEADS, -1).transpose(1, 0, 2)

def join_heads(stacked):
    return stacked.transpose(1, 0, 2).reshape(stacked.shape[1], -1)

def head_forward(operands, allowed):
    queries_head, keys_head, values_head = operands
    factor = 1.0 / math.sqrt(queries_head.shape[1])
    scores = product_right(queries_head, keys_head) * factor
    masked = jnp.where(allowed, scores, -1e+30)
    highest = lax.optimization_barrier(jnp.max(masked, axis=1, keepdims=True))
    log_total = highest + jnp.log(lax.optimization_barrier(jnp.sum(jnp.exp(masked - highest), axis=1, keepdims=True)))
    weights = jnp.where(allowed, jnp.exp(masked - log_total), 0.0)
    attended = product(weights.astype(jnp.bfloat16), values_head).astype(jnp.bfloat16)
    return (attended, log_total[:, 0])

def head_backward(operands, allowed):
    queries_head, keys_head, values_head, grad_head, attended, log_total = operands
    factor = 1.0 / math.sqrt(queries_head.shape[1])
    scores = product_right(queries_head, keys_head) * factor
    masked = jnp.where(allowed, scores, -1e+30)
    weights = jnp.where(allowed, jnp.exp(masked - log_total[:, None]), 0.0)
    weights_low = weights.astype(jnp.bfloat16)
    row_dot = lax.optimization_barrier(jnp.sum(grad_head.astype(jnp.float32) * attended.astype(jnp.float32), axis=1, keepdims=True))
    grad_weights = product_right(grad_head, values_head)
    grad_scores = (weights * (grad_weights - row_dot)).astype(jnp.bfloat16)
    grad_query = product(grad_scores, keys_head) * factor
    grad_keys = product_left(grad_scores, queries_head) * factor
    grad_values = product_left(weights_low, grad_head)
    return (grad_query, grad_keys, grad_values)

def reference(hidden_in, segment_ids, span_order, qkv_weight, out_weight, up_weight, down_weight, vectors, cotangent):
    vector_wide = vectors.astype(jnp.float32)
    gain_one = vector_wide[0]
    bias_one = vector_wide[1]
    bias_query = vector_wide[2]
    bias_value = vector_wide[3]
    bias_out = vector_wide[4]
    gain_two = vector_wide[5]
    bias_two = vector_wide[6]
    bias_down = vector_wide[7]
    bias_up = vector_wide[8:12].reshape(-1)

    def sequence_step(totals_in, inputs):
        rows_in, grad_rows, segment_row, order_row = inputs
        offsets = jnp.arange(TOK_DEV, dtype=jnp.int32)
        positions = (order_row[:, None] * TOK_DEV + offsets[None, :]).reshape(-1).astype(jnp.int32)
        segment_here = jnp.take(segment_row, positions)
        allowed = (positions[None, :] <= positions[:, None]) & (segment_here[None, :] == segment_here[:, None])
        normed_one, inverse_one = normalize(rows_in)
        attn_in = (normed_one * gain_one + bias_one).astype(jnp.bfloat16)
        projected = product(attn_in, qkv_weight)
        queries = (projected[:, :D] + bias_query).astype(jnp.bfloat16)
        keys_all = projected[:, D:2 * D].astype(jnp.bfloat16)
        values_all = (projected[:, 2 * D:] + bias_value).astype(jnp.bfloat16)
        heads_query = split_heads(queries)
        heads_key = split_heads(keys_all)
        heads_value = split_heads(values_all)
        attended_heads, log_totals = lax.map(partial(head_forward, allowed=allowed), (heads_query, heads_key, heads_value))
        attended = join_heads(attended_heads)
        middle = rows_in + product(attended, out_weight) + bias_out
        normed_two, inverse_two = normalize(middle)
        ffn_in = (normed_two * gain_two + bias_two).astype(jnp.bfloat16)
        activated, derivative = gelu_pair(product(ffn_in, up_weight) + bias_up)
        act_low = activated.astype(jnp.bfloat16)
        block_rows = middle + product(act_low, down_weight) + bias_down
        grad_low = grad_rows.astype(jnp.bfloat16)
        grad_pre = product_right(grad_low, down_weight) * derivative
        grad_pre_low = grad_pre.astype(jnp.bfloat16)
        grad_ffn_in = product_right(grad_pre_low, up_weight)
        grad_middle = grad_rows + norm_back(grad_ffn_in, normed_two, inverse_two, gain_two)
        grad_middle_low = grad_middle.astype(jnp.bfloat16)
        grad_attended = product_right(grad_middle_low, out_weight).astype(jnp.bfloat16)
        grads_query, grads_key, grads_value = lax.map(partial(head_backward, allowed=allowed), (heads_query, heads_key, heads_value, split_heads(grad_attended), attended_heads, log_totals))
        grad_queries = join_heads(grads_query)
        grad_values = join_heads(grads_value)
        grad_projected_low = jnp.concatenate([grad_queries, join_heads(grads_key), grad_values], axis=1).astype(jnp.bfloat16)
        grad_attn_in = product_right(grad_projected_low, qkv_weight)
        grad_input = grad_middle + norm_back(grad_attn_in, normed_one, inverse_one, gain_one)
        vector_terms = jnp.concatenate([jnp.stack([lax.optimization_barrier(jnp.sum(grad_attn_in * normed_one, axis=0)), lax.optimization_barrier(jnp.sum(grad_attn_in, axis=0)), lax.optimization_barrier(jnp.sum(grad_queries, axis=0)), lax.optimization_barrier(jnp.sum(grad_values, axis=0)), lax.optimization_barrier(jnp.sum(grad_middle, axis=0)), lax.optimization_barrier(jnp.sum(grad_ffn_in * normed_two, axis=0)), lax.optimization_barrier(jnp.sum(grad_ffn_in, axis=0)), lax.optimization_barrier(jnp.sum(grad_rows, axis=0))]), lax.optimization_barrier(jnp.sum(grad_pre, axis=0)).reshape(4, D)], axis=0)
        totals_out = (totals_in[0] + product_left(attn_in, grad_projected_low), totals_in[1] + product_left(attended, grad_middle_low), totals_in[2] + product_left(ffn_in, grad_pre_low), totals_in[3] + product_left(act_low, grad_low), totals_in[4] + vector_terms)
        return (totals_out, (block_rows, grad_input))
    start_totals = (jnp.zeros((D, 3 * D), jnp.float32), jnp.zeros((D, D), jnp.float32), jnp.zeros((D, FF), jnp.float32), jnp.zeros((FF, D), jnp.float32), jnp.zeros((12, D), jnp.float32))
    totals, (block_all, grad_all) = lax.scan(sequence_step, start_totals, (hidden_in.reshape(SEQS, LEN, D), cotangent.reshape(SEQS, LEN, D), segment_ids, span_order))
    return (block_all.reshape(TOKENS, D), grad_all.reshape(TOKENS, D), totals[0], totals[1], totals[2], totals[3], totals[4])
```

```python
from functools import partial
import math

import jax
import jax.numpy as jnp
from jax import lax
from jax.experimental import pallas as pl
from jax.experimental.pallas import tpu as pltpu
from jax.sharding import PartitionSpec as P

HEADS = 25


eps_norm = 1e-05
gelu_c = math.sqrt(2.0 / math.pi)
f32 = jnp.float32
bf16 = jnp.bfloat16


def product(left_side, right_side):
    return jnp.dot(left_side, right_side, preferred_element_type=f32)


def product_left(left_side, right_side):
    return lax.dot_general(
        left_side, right_side, (((0,), (0,)), ((), ())), preferred_element_type=f32
    )


def product_right(left_side, right_side):
    return lax.dot_general(
        left_side, right_side, (((1,), (1,)), ((), ())), preferred_element_type=f32
    )


def normalize(inputs):
    average = jnp.mean(inputs, axis=1, keepdims=True)
    centred = inputs - average
    inverse = lax.rsqrt(jnp.mean(centred * centred, axis=1, keepdims=True) + eps_norm)
    return (centred * inverse, inverse)


def norm_back(upstream, normed, inverse, gain_row):
    scaled = upstream * gain_row
    return inverse * (
        scaled
        - jnp.mean(scaled, axis=1, keepdims=True)
        - normed * jnp.mean(scaled * normed, axis=1, keepdims=True)
    )


def gelu_pair(preact):
    tangent = jnp.tanh(gelu_c * (preact + 0.044715 * preact * preact * preact))
    activated = 0.5 * preact * (1.0 + tangent)
    derivative = 0.5 * (1.0 + tangent) + 0.5 * preact * (1.0 - tangent * tangent) * gelu_c * (
        1.0 + 0.134145 * preact * preact
    )
    return (activated, derivative)


def allowed_pairs(pos_col, pos_row, seg_col, seg_row):
    return (pos_row[...] <= pos_col[...]) & (seg_row[...] == seg_col[...])


def attend_kernel(
    window, depth, own_ref, pos_col, pos_row, seg_col, seg_row, q_ref, k_ref, v_ref, o_ref, own_o_ref, lse_ref
):
    allowed = allowed_pairs(pos_col, pos_row, seg_col, seg_row)
    factor = 1.0 / math.sqrt(depth)
    for head in range(window):
        columns = slice(head * depth, (head + 1) * depth)
        scores = product_right(q_ref[:, columns], k_ref[:, columns]) * factor
        masked = jnp.where(allowed, scores, -1e30)
        highest = jnp.max(masked, axis=1, keepdims=True)
        raised = jnp.exp(masked - highest)
        total = jnp.sum(raised, axis=1, keepdims=True)
        weights = (raised * (1.0 / total)).astype(bf16)
        attended = product(weights, v_ref[:, columns])
        o_ref[:, columns] = attended.astype(bf16)
        lse_ref[:, head : head + 1] = highest + jnp.log(total)
    first = own_ref[0]
    column = lax.broadcasted_iota(jnp.int32, o_ref.shape, 1)
    inside = (column >= first) & (column < first + own_ref[1])
    own_o_ref[...] = jnp.where(inside, o_ref[...].astype(f32), 0.0).astype(bf16)


def attend_back_kernel(
    window,
    depth,
    own_ref,
    pos_col,
    pos_row,
    seg_col,
    seg_row,
    q_ref,
    k_ref,
    v_ref,
    o_ref,
    go_ref,
    lse_ref,
    gp_ref,
    sums_ref,
):
    allowed = allowed_pairs(pos_col, pos_row, seg_col, seg_row)
    factor = 1.0 / math.sqrt(depth)
    width = window * depth
    first = own_ref[0]
    last = first + own_ref[1]
    for head in range(window):
        columns = slice(head * depth, (head + 1) * depth)
        queries, keys, values = q_ref[:, columns], k_ref[:, columns], v_ref[:, columns]
        grad_head = go_ref[:, columns]
        scores = product_right(queries, keys) * factor
        weights = jnp.where(allowed, jnp.exp(scores - lse_ref[:, head : head + 1]), 0.0)
        row_dot = jnp.sum(
            grad_head.astype(f32) * o_ref[:, columns].astype(f32), axis=1, keepdims=True
        )
        grad_weights = product_right(grad_head, values)
        grad_scores = (weights * (grad_weights - row_dot)).astype(bf16)
        grad_query = product(grad_scores, keys) * factor
        grad_keys = product_left(grad_scores, queries) * factor
        grad_values = product_left(weights.astype(bf16), grad_head)
        column = lax.broadcasted_iota(jnp.int32, (1, depth), 1) + head * depth
        inside = (column >= first) & (column < last)
        for place, grad in enumerate((grad_query, grad_keys, grad_values)):
            own = jnp.where(inside, grad, 0.0)
            where_to = slice(place * width + head * depth, place * width + (head + 1) * depth)
            gp_ref[:, where_to] = own.astype(bf16)
            sums_ref[:, where_to] = jnp.sum(own, axis=0, keepdims=True)


def on_device(
    sizes,
    hidden_in,
    segment_ids,
    span_order,
    qkv_weight,
    out_weight,
    up_weight,
    down_weight,
    vectors,
    cotangent,
):
    n_rep, n_shard = sizes
    tokens_here, model_width = hidden_in.shape
    depth = model_width // HEADS
    rows_own = model_width // n_shard
    ff_own = down_weight.shape[0]
    length = tokens_here * n_shard
    me = lax.axis_index("shard")
    rep = lax.axis_index("rep")
    core = rep % 2
    line = rep // 2
    n_line = n_rep // 2

    windows = [
        (i * rows_own // depth, -(-(i + 1) * rows_own // depth)) for i in range(n_shard)
    ]
    window = max(stop - start for start, stop in windows)
    starts = [min(start, HEADS - window) for start, _ in windows]
    width = window * depth
    offsets = [i * rows_own - starts[i] * depth for i in range(n_shard)]
    own_offset = jnp.asarray(offsets, jnp.int32)[me]

    def xor(d):
        return [(i, i ^ d) for i in range(n_shard)]

    def swap(parts):
        return [parts[0]] + [
            lax.ppermute(parts[d], "shard", xor(d)) for d in range(1, n_shard)
        ]

    def gather(part):
        return jnp.concatenate(swap([part] * n_shard), axis=0)

    def scatter_sum(total):
        pieces = total.astype(bf16).reshape(n_shard, tokens_here, -1)
        got = swap([pieces[d] for d in range(n_shard)])
        return sum(piece.astype(f32) for piece in got[1:]) + got[0].astype(f32)

    def pick(stacked, index):
        return lax.dynamic_index_in_dim(stacked, index, 0, keepdims=False)

    def partner(part):
        return lax.ppermute(part, "rep", [(i, i ^ 1) for i in range(n_rep)])

    def by_core(mine, other, axis):
        first = jnp.where(core == 0, mine, other)
        second = jnp.where(core == 0, other, mine)
        return jnp.concatenate([first, second], axis=axis)

    def by_place(parts):
        stacked = jnp.stack(parts)
        return [pick(stacked, me ^ j) for j in range(n_shard)]

    def reshard(stacked):
        c = stacked.shape[2]
        half = rows_own // 2
        mine = [
            lax.dynamic_slice(stacked, (me ^ d, half * core, 0), (1, half, c))[0]
            for d in range(n_shard)
        ]
        got = jnp.stack(swap(mine)[1:])
        both = by_core(got, partner(got), 1)
        parts = [pick(stacked, me)] + [both[d] for d in range(n_shard - 1)]
        return jnp.concatenate(by_place(parts), axis=0)

    def line_pairs(members, step):
        return [
            (2 * q + c, 2 * (q + step) + c) for q in members for c in range(2)
        ]

    def line_sum(part):
        rows, c = part.shape
        padded = -(-rows // n_line) * n_line
        if padded != rows:
            part = jnp.pad(part, ((0, padded - rows), (0, 0)))
        chunks = part.reshape(n_line, padded // n_line, c)
        mirrored = n_line - 1 - line
        right = left = None
        for t in range(1, n_line):
            own_right = pick(chunks, jnp.clip(n_line - t + line, 0, n_line - 1))
            own_left = pick(chunks, jnp.clip(t - 1 - mirrored, 0, n_line - 1))
            if t > 1:
                own_right = (own_right.astype(f32) + right.astype(f32)).astype(bf16)
                own_left = (own_left.astype(f32) + left.astype(f32)).astype(bf16)
            right = lax.ppermute(own_right, "rep", line_pairs(range(t), 1))
            left = lax.ppermute(
                own_left, "rep", line_pairs([n_line - 1 - q for q in range(t)], -1)
            )
        own = pick(chunks, line).astype(f32) + right.astype(f32) + left.astype(f32)
        own = own.astype(bf16)
        rights, lefts = [own], [own]
        for t in range(1, n_line):
            members = range(t - 1, n_line - 1)
            rights.append(lax.ppermute(rights[-1], "rep", line_pairs(members, 1)))
            lefts.append(
                lax.ppermute(
                    lefts[-1], "rep", line_pairs([n_line - 1 - q for q in members], -1)
                )
            )
        around = jnp.stack(rights[:0:-1] + [own] + lefts[1:])
        total = lax.dynamic_slice_in_dim(around, n_line - 1 - line, n_line, 0)
        return total.reshape(padded, c)[:rows]

    def reduce_rows(term):
        halves = term.astype(bf16).reshape(2, term.shape[0] // 2, term.shape[1])
        got = partner(pick(halves, 1 - core))
        mine = (pick(halves, core).astype(f32) + got.astype(f32)).astype(bf16)
        mine = line_sum(mine)
        return by_core(mine, partner(mine), 0).astype(f32)

    def reduce_columns(term):
        c = term.shape[1]
        half = rows_own // 2
        halves = term.astype(bf16).reshape(n_shard, 2, half, c)
        sent = lax.dynamic_slice_in_dim(halves, 1 - core, 1, 1)[:, 0]
        kept = lax.dynamic_slice_in_dim(halves, core, 1, 1)[:, 0]
        mine = (kept.astype(f32) + partner(sent).astype(f32)).astype(bf16)
        got = jnp.concatenate(swap([pick(mine, me ^ d) for d in range(n_shard)]), axis=0)
        mine = line_sum(got).reshape(n_shard, half, c)
        both = by_core(mine, partner(mine), 1)
        return [pick(both, me ^ j) for j in range(n_shard)]

    vector_parts = swap([vectors] * n_shard)
    vector_wide = jnp.concatenate(by_place(vector_parts), axis=1).astype(f32)
    gain_one = vector_wide[0]
    bias_one = vector_wide[1]
    bias_out = vector_wide[4]
    gain_two = vector_wide[5]
    bias_two = vector_wide[6]
    bias_down = vector_wide[7]
    bias_up = pick(vector_wide[8:12].reshape(n_shard, ff_own), me)
    spans = jnp.stack(
        [
            vector_wide[2:4, start * depth : start * depth + width]
            for start in starts
        ]
    )
    bias_query, bias_value = pick(spans, me)

    order_row = span_order[0]
    within = jnp.arange(tokens_here, dtype=jnp.int32)
    firsts = [order_row[me ^ d] * tokens_here for d in range(n_shard)]
    pos = jnp.concatenate([first + within for first in firsts])
    seg = jnp.concatenate(
        [lax.dynamic_slice(segment_ids[0], (first,), (tokens_here,)) for first in firsts]
    )
    mask_args = (pos[:, None], pos[None, :], seg[:, None], seg[None, :])
    own_args = jnp.stack([own_offset, jnp.int32(rows_own)])

    normed_one, inverse_one = normalize(hidden_in)
    attn_in = (normed_one * gain_one + bias_one).astype(bf16)
    attn_all = gather(attn_in)
    qkv_cut = jnp.stack(
        [
            jnp.concatenate(
                [
                    qkv_weight[:, p * model_width + s * depth : p * model_width + s * depth + width]
                    for p in range(3)
                ],
                axis=1,
            )
            for s in starts
        ]
    )
    qkv_here = reshard(qkv_cut)
    up_cut = up_weight.reshape(rows_own, n_shard, ff_own).transpose(1, 0, 2)
    up_here = reshard(up_cut)
    edge = depth
    to_next = [(i, i + 1) for i in range(n_shard - 1)]
    to_last = [(i + 1, i) for i in range(n_shard - 1)]
    out_long = jnp.concatenate(
        [
            lax.ppermute(out_weight[rows_own - edge :], "shard", to_next),
            out_weight,
            lax.ppermute(out_weight[:edge], "shard", to_last),
        ],
        axis=0,
    )
    out_here = lax.dynamic_slice_in_dim(out_long, edge - own_offset, width, 0)

    grad_low = cotangent.astype(bf16)

    projected = product(attn_all, qkv_here)
    queries = (projected[:, :width] + bias_query).astype(bf16)
    keys = projected[:, width : 2 * width].astype(bf16)
    values = (projected[:, 2 * width :] + bias_value).astype(bf16)

    vmem = pl.BlockSpec(memory_space=pltpu.VMEM)
    smem = pl.BlockSpec(memory_space=pltpu.SMEM)
    params = pltpu.CompilerParams(vmem_limit_bytes=60 * 1024 * 1024)
    attended, attended_own, log_totals = pl.pallas_call(
        partial(attend_kernel, window, depth),
        in_specs=[smem] + [vmem] * 7,
        out_specs=[vmem] * 3,
        out_shape=(
            jax.ShapeDtypeStruct((length, width), bf16),
            jax.ShapeDtypeStruct((length, width), bf16),
            jax.ShapeDtypeStruct((length, window), f32),
        ),
        compiler_params=params,
        name="attend",
    )(own_args, *mask_args, queries, keys, values)

    middle = hidden_in + scatter_sum(product(attended_own, out_here)) + bias_out
    normed_two, inverse_two = normalize(middle)
    ffn_in = (normed_two * gain_two + bias_two).astype(bf16)
    ffn_all = gather(ffn_in)
    activated, derivative = gelu_pair(product(ffn_all, up_here) + bias_up)
    act_low = activated.astype(bf16)
    block_out = middle + scatter_sum(product(act_low, down_weight)) + bias_down

    grad_all = gather(grad_low)
    grad_pre = product_right(grad_all, down_weight) * derivative
    grad_pre_low = grad_pre.astype(bf16)
    down_grad = reduce_rows(product_left(act_low, grad_all))
    grad_ffn_in = scatter_sum(product_right(grad_pre_low, up_here))
    up_places = reduce_columns(product_left(ffn_all, grad_pre_low))
    up_grad = jnp.concatenate(up_places, axis=1).astype(f32)

    grad_middle = cotangent + norm_back(grad_ffn_in, normed_two, inverse_two, gain_two)
    middle_all = gather(grad_middle.astype(bf16))
    grad_attended = product_right(middle_all, out_here).astype(bf16)
    out_term = lax.dynamic_slice_in_dim(
        product_left(attended_own, middle_all), own_offset, rows_own, 0
    )
    out_grad = reduce_rows(out_term)

    grad_projected, head_sums = pl.pallas_call(
        partial(attend_back_kernel, window, depth),
        in_specs=[smem] + [vmem] * 10,
        out_specs=[vmem] * 2,
        out_shape=(
            jax.ShapeDtypeStruct((length, 3 * width), bf16),
            jax.ShapeDtypeStruct((1, 3 * width), f32),
        ),
        compiler_params=params,
        name="attend_back",
    )(own_args, *mask_args, queries, keys, values, attended, grad_attended, log_totals)

    qkv_places = reduce_columns(product_left(attn_all, grad_projected))
    qkv_grad = jnp.concatenate(
        [
            qkv_places[j][:, p * width + offsets[j] : p * width + offsets[j] + rows_own]
            for p in range(3)
            for j in range(n_shard)
        ],
        axis=1,
    ).astype(f32)
    grad_attn_in = scatter_sum(product_right(grad_projected, qkv_here))
    input_grad = grad_middle + norm_back(grad_attn_in, normed_one, inverse_one, gain_one)

    head_first = jnp.asarray([s * depth for s in starts], jnp.int32)[me]
    blank = jnp.zeros((1, model_width), f32)
    query_sums = lax.dynamic_update_slice(blank, head_sums[:, :width], (0, head_first))
    value_sums = lax.dynamic_update_slice(blank, head_sums[:, 2 * width :], (0, head_first))
    pre_sums = lax.dynamic_update_slice(
        jnp.zeros((n_shard, ff_own), f32), jnp.sum(grad_pre, axis=0)[None], (me, 0)
    ).reshape(4, model_width)
    vector_terms = jnp.concatenate(
        [
            jnp.stack(
                [jnp.sum(grad_attn_in * normed_one, axis=0), jnp.sum(grad_attn_in, axis=0)]
            ),
            query_sums,
            value_sums,
            jnp.stack(
                [
                    jnp.sum(grad_middle, axis=0),
                    jnp.sum(grad_ffn_in * normed_two, axis=0),
                    jnp.sum(grad_ffn_in, axis=0),
                    jnp.sum(cotangent, axis=0),
                ]
            ),
            pre_sums,
        ],
        axis=0,
    )
    vector_cut = vector_terms.reshape(12, n_shard, rows_own).transpose(1, 0, 2)
    vector_grad = sum(swap([pick(vector_cut, me ^ d) for d in range(n_shard)]))
    step = 1
    while step < n_rep:
        vector_grad = vector_grad + lax.ppermute(
            vector_grad, "rep", [(i, i ^ step) for i in range(n_rep)]
        )
        step *= 2
    return (block_out, input_grad, qkv_grad, out_grad, up_grad, down_grad, vector_grad)


def solution(mesh):
    placed = (
        P(("rep", "shard"), None),
        P("rep", None),
        P("rep", None),
        P("shard", None),
        P("shard", None),
        P("shard", None),
        P("shard", None),
        P(None, "shard"),
        P(("rep", "shard"), None),
    )
    return jax.shard_map(
        partial(on_device, (mesh.shape["rep"], mesh.shape["shard"])),
        mesh=mesh,
        in_specs=placed,
        out_specs=(
            P(("rep", "shard"), None),
            P(("rep", "shard"), None),
            P("shard", None),
            P("shard", None),
            P("shard", None),
            P("shard", None),
            P(None, "shard"),
        ),
        check_vma=False,
    )
```

```python
from functools import partial
import math

import jax
import jax.numpy as jnp
from jax import lax
from jax.experimental import pallas as pl
from jax.experimental.pallas import tpu as pltpu
from jax.sharding import PartitionSpec as P

HEADS = 25


eps_norm = 1e-05
gelu_c = math.sqrt(2.0 / math.pi)
f32 = jnp.float32
bf16 = jnp.bfloat16


def product(left_side, right_side):
    return jnp.dot(left_side, right_side, preferred_element_type=f32)


def product_left(left_side, right_side):
    return lax.dot_general(
        left_side, right_side, (((0,), (0,)), ((), ())), preferred_element_type=f32
    )


def product_right(left_side, right_side):
    return lax.dot_general(
        left_side, right_side, (((1,), (1,)), ((), ())), preferred_element_type=f32
    )


def normalize(inputs):
    average = jnp.mean(inputs, axis=1, keepdims=True)
    centred = inputs - average
    inverse = lax.rsqrt(jnp.mean(centred * centred, axis=1, keepdims=True) + eps_norm)
    return (centred * inverse, inverse)


def norm_back(upstream, normed, inverse, gain_row):
    scaled = upstream * gain_row
    return inverse * (
        scaled
        - jnp.mean(scaled, axis=1, keepdims=True)
        - normed * jnp.mean(scaled * normed, axis=1, keepdims=True)
    )


def gelu_pair(preact):
    tangent = jnp.tanh(gelu_c * (preact + 0.044715 * preact * preact * preact))
    activated = 0.5 * preact * (1.0 + tangent)
    derivative = 0.5 * (1.0 + tangent) + 0.5 * preact * (1.0 - tangent * tangent) * gelu_c * (
        1.0 + 0.134145 * preact * preact
    )
    return (activated, derivative)


def allowed_pairs(pos_col, pos_row, seg_col, seg_row):
    return (pos_row[...] <= pos_col[...]) & (seg_row[...] == seg_col[...])


def cut_kernel(n_shard, columns, at_ref, w_ref, sent_ref, own_ref):
    me, core = at_ref[0], at_ref[1]
    rows = w_ref.shape[0]
    half = rows // 2

    def one(d, carry):
        for j in range(n_shard):
            for c in range(2):

                @pl.when((me ^ d == j) & (core == c))
                def _():
                    for start, to, size in columns[j]:
                        sent_ref[d - 1, :, to : to + size] = w_ref[
                            c * half : (c + 1) * half, start : start + size
                        ]

        return carry

    lax.fori_loop(1, n_shard, one, 0)
    for j in range(n_shard):

        @pl.when(me == j)
        def _():
            for start, to, size in columns[j]:
                own_ref[:, to : to + size] = w_ref[:, start : start + size]


def place_kernel(n_places, columns, at_ref, mine_ref, other_ref, out_ref):
    me, core = at_ref[0], at_ref[1]
    half = out_ref.shape[0] // 2

    def one(d, carry):
        for j in range(n_places):
            for c in range(2):

                @pl.when((me ^ d == j) & (core == c))
                def _():
                    for start, to, size in columns[j]:
                        out_ref[c * half : (c + 1) * half, to : to + size] = mine_ref[
                            d, :, start : start + size
                        ].astype(f32)
                        out_ref[(1 - c) * half : (2 - c) * half, to : to + size] = other_ref[
                            d, :, start : start + size
                        ].astype(f32)

        return carry

    lax.fori_loop(0, n_places, one, 0)


def assemble(n_shard, at_ref, own_ref, mine_ref, other_ref, full_ref):
    me, core = at_ref[0], at_ref[1]
    rows = own_ref.shape[0]
    half = rows // 2
    for j in range(n_shard):
        first = j * rows

        @pl.when(me == j)
        def _():
            full_ref[first : first + rows, :] = own_ref[...]

        for c in range(2):

            @pl.when((me != j) & (core == c))
            def _():
                d = (me ^ j) - 1
                full_ref[first + c * half : first + (c + 1) * half, :] = mine_ref[d]
                full_ref[first + (1 - c) * half : first + (2 - c) * half, :] = other_ref[d]


def attend_kernel(
    n_shard,
    window,
    depth,
    at_ref,
    pos_col,
    pos_row,
    seg_col,
    seg_row,
    h_ref,
    own_w,
    mine_w,
    other_w,
    bias_ref,
    out_w,
    w_ref,
    qkv_ref,
    o_ref,
    own_o_ref,
    lse_ref,
    part_ref,
):
    assemble(n_shard, at_ref, own_w, mine_w, other_w, w_ref)
    qkv_ref[...] = (product(h_ref[...], w_ref[...]) + bias_ref[...]).astype(bf16)
    allowed = allowed_pairs(pos_col, pos_row, seg_col, seg_row)
    factor = 1.0 / math.sqrt(depth)
    width = window * depth
    for head in range(window):
        q_at, k_at, v_at = (
            slice(p * width + head * depth, p * width + (head + 1) * depth) for p in range(3)
        )
        scores = product_right(qkv_ref[:, q_at], qkv_ref[:, k_at]) * factor
        masked = jnp.where(allowed, scores, -1e30)
        highest = jnp.max(masked, axis=1, keepdims=True)
        raised = jnp.exp(masked - highest)
        total = jnp.sum(raised, axis=1, keepdims=True)
        weights = (raised * (1.0 / total)).astype(bf16)
        attended = product(weights, qkv_ref[:, v_at])
        o_ref[:, q_at] = attended.astype(bf16)
        lse_ref[:, head : head + 1] = highest + jnp.log(total)
    first = at_ref[2]
    column = lax.broadcasted_iota(jnp.int32, o_ref.shape, 1)
    inside = (column >= first) & (column < first + at_ref[3])
    own_o_ref[...] = jnp.where(inside, o_ref[...].astype(f32), 0.0).astype(bf16)
    part_ref[...] = product(own_o_ref[...], out_w[...]).astype(bf16)


def feed_kernel(
    n_shard,
    at_ref,
    h_ref,
    own_w,
    mine_w,
    other_w,
    bias_ref,
    down_ref,
    y_ref,
    act_ref,
    low_ref,
    part_ref,
    sums_ref,
    w_ref,
):
    assemble(n_shard, at_ref, own_w, mine_w, other_w, w_ref)
    activated, derivative = gelu_pair(product(h_ref[...], w_ref[...]) + bias_ref[...])
    act_ref[...] = activated.astype(bf16)
    grad_pre = product_right(y_ref[...], down_ref[...]) * derivative
    sums_ref[...] = jnp.sum(grad_pre, axis=0, keepdims=True)
    low_ref[...] = grad_pre.astype(bf16)
    part_ref[...] = product_right(low_ref[...], w_ref[...]).astype(bf16)


def attend_back_kernel(
    window,
    depth,
    at_ref,
    pos_col,
    pos_row,
    seg_col,
    seg_row,
    qkv_ref,
    o_ref,
    go_ref,
    lse_ref,
    gp_ref,
    sums_ref,
):
    allowed = allowed_pairs(pos_col, pos_row, seg_col, seg_row)
    factor = 1.0 / math.sqrt(depth)
    width = window * depth
    first = at_ref[2]
    last = first + at_ref[3]
    for head in range(window):
        columns = slice(head * depth, (head + 1) * depth)
        queries, keys, values = (
            qkv_ref[:, p * width + head * depth : p * width + (head + 1) * depth]
            for p in range(3)
        )
        grad_head = go_ref[:, columns]
        scores = product_right(queries, keys) * factor
        weights = jnp.where(allowed, jnp.exp(scores - lse_ref[:, head : head + 1]), 0.0)
        row_dot = jnp.sum(
            grad_head.astype(f32) * o_ref[:, columns].astype(f32), axis=1, keepdims=True
        )
        grad_weights = product_right(grad_head, values)
        grad_scores = (weights * (grad_weights - row_dot)).astype(bf16)
        grad_query = product(grad_scores, keys) * factor
        grad_keys = product_left(grad_scores, queries) * factor
        grad_values = product_left(weights.astype(bf16), grad_head)
        column = lax.broadcasted_iota(jnp.int32, (1, depth), 1) + head * depth
        inside = (column >= first) & (column < last)
        for place, grad in enumerate((grad_query, grad_keys, grad_values)):
            own = jnp.where(inside, grad, 0.0)
            where_to = slice(place * width + head * depth, place * width + (head + 1) * depth)
            gp_ref[:, where_to] = own.astype(bf16)
            sums_ref[:, where_to] = jnp.sum(own, axis=0, keepdims=True)


def on_device(
    sizes,
    hidden_in,
    segment_ids,
    span_order,
    qkv_weight,
    out_weight,
    up_weight,
    down_weight,
    vectors,
    cotangent,
):
    n_rep, n_shard = sizes
    tokens_here, model_width = hidden_in.shape
    depth = model_width // HEADS
    rows_own = model_width // n_shard
    ff_own = down_weight.shape[0]
    length = tokens_here * n_shard
    me = lax.axis_index("shard")
    rep = lax.axis_index("rep")
    core = rep % 2
    line = rep // 2
    n_line = n_rep // 2

    windows = [
        (i * rows_own // depth, -(-(i + 1) * rows_own // depth)) for i in range(n_shard)
    ]
    window = max(stop - start for start, stop in windows)
    starts = [min(start, HEADS - window) for start, _ in windows]
    width = window * depth
    offsets = [i * rows_own - starts[i] * depth for i in range(n_shard)]
    own_offset = jnp.asarray(offsets, jnp.int32)[me]

    tie = lax.optimization_barrier

    def xor(d):
        return [(i, i ^ d) for i in range(n_shard)]

    def swap(parts):
        return [parts[0]] + [
            lax.ppermute(parts[d], "shard", xor(d)) for d in range(1, n_shard)
        ]

    def gather(part):
        return jnp.concatenate(swap([part] * n_shard), axis=0)

    def scatter_sum(total):
        pieces = total.astype(bf16).reshape(n_shard, tokens_here, -1)
        got = swap([pieces[d] for d in range(n_shard)])
        return sum(piece.astype(f32) for piece in got[1:]) + got[0].astype(f32)

    def pick(stacked, index):
        return lax.dynamic_index_in_dim(stacked, index, 0, keepdims=False)

    def partner(part):
        return lax.ppermute(part, "rep", [(i, i ^ 1) for i in range(n_rep)])

    def by_place(parts):
        stacked = jnp.stack(parts)
        return [pick(stacked, me ^ j) for j in range(n_shard)]

    vmem = pl.BlockSpec(memory_space=pltpu.VMEM)
    smem = pl.BlockSpec(memory_space=pltpu.SMEM)
    params = pltpu.CompilerParams(vmem_limit_bytes=60 * 1024 * 1024)
    at = jnp.stack([me, core, own_offset, jnp.int32(rows_own)]).astype(jnp.int32)

    def call(body, n_in, shapes, name, scratch=()):
        return pl.pallas_call(
            body,
            in_specs=[smem] + [vmem] * n_in,
            out_specs=[vmem] * len(shapes),
            out_shape=[jax.ShapeDtypeStruct(*shape) for shape in shapes],
            scratch_shapes=scratch,
            compiler_params=params,
            name=name,
        )

    def reshard(weight, columns, size, name):
        half = rows_own // 2
        sent, own = call(
            partial(cut_kernel, n_shard, columns),
            1,
            [((n_shard - 1, half, size), bf16), ((rows_own, size), bf16)],
            name,
        )(at, weight)
        mine = jnp.stack(swap([None] + [sent[d] for d in range(n_shard - 1)])[1:])
        return own, mine, partner(mine)

    def place(pieces, others, columns, total, name):
        return call(
            partial(place_kernel, len(columns), columns),
            2,
            [((2 * pieces.shape[1], total), f32)],
            name,
        )(at if len(columns) > 1 else at.at[0].set(0), pieces, others)[0]

    def hop(part, hops):
        return lax.ppermute(
            part, "rep", [(2 * a + c, 2 * b + c) for a, b in hops for c in range(2)]
        )

    inner = n_line // 2

    def line_sum(part):
        stages = []
        for s in range(inner - 1):
            got = hop(part, [(s, s + 1), (n_line - 1 - s, n_line - 2 - s)])
            part = (part.astype(f32) + got.astype(f32)).astype(bf16)
            stages.append(got)
        got = hop(part, [(inner - 1, inner), (inner, inner - 1)])
        total = (part.astype(f32) + got.astype(f32)).astype(bf16)
        stages.append(got)
        for s in reversed(range(inner - 1)):
            got = hop(total, [(s + 1, s), (n_line - 2 - s, n_line - 1 - s)])
            outside = (line <= s) | (line >= n_line - 1 - s)
            total = jnp.where(outside, got, total)
        stages.append(total)
        return stages

    def core_rows(term):
        halves = term.astype(bf16).reshape(2, term.shape[0] // 2, term.shape[1])
        got = partner(pick(halves, 1 - core))
        return (pick(halves, core).astype(f32) + got.astype(f32)).astype(bf16)

    def core_columns(term):
        c = term.shape[1]
        halves = term.astype(bf16).reshape(n_shard, 2, rows_own // 2, c)
        sent = lax.dynamic_slice_in_dim(halves, 1 - core, 1, 1)[:, 0]
        kept = lax.dynamic_slice_in_dim(halves, core, 1, 1)[:, 0]
        return (kept.astype(f32) + partner(sent).astype(f32)).astype(bf16)

    def to_owners(mine):
        return swap([pick(mine, me ^ d) for d in range(n_shard)])

    vector_parts = swap([vectors] * n_shard)
    vector_wide = jnp.concatenate(by_place(vector_parts), axis=1).astype(f32)
    gain_one = vector_wide[0]
    bias_one = vector_wide[1]
    bias_out = vector_wide[4]
    gain_two = vector_wide[5]
    bias_two = vector_wide[6]
    bias_down = vector_wide[7]
    bias_up = pick(vector_wide[8:12].reshape(n_shard, ff_own), me)
    spans = jnp.stack(
        [
            vector_wide[2:4, start * depth : start * depth + width]
            for start in starts
        ]
    )
    bias_query, bias_value = pick(spans, me)

    order_row = span_order[0]
    within = jnp.arange(tokens_here, dtype=jnp.int32)
    firsts = [order_row[me ^ d] * tokens_here for d in range(n_shard)]
    pos = jnp.concatenate([first + within for first in firsts])
    seg = jnp.concatenate(
        [lax.dynamic_slice(segment_ids[0], (first,), (tokens_here,)) for first in firsts]
    )
    mask_args = (pos[:, None], pos[None, :], seg[:, None], seg[None, :])

    normed_one, inverse_one = normalize(hidden_in)
    attn_in = (normed_one * gain_one + bias_one).astype(bf16)
    attn_all = gather(attn_in)
    qkv_columns = [
        [(p * model_width + starts[j] * depth, p * width, width) for p in range(3)]
        for j in range(n_shard)
    ]
    qkv_weights = reshard(qkv_weight, qkv_columns, 3 * width, "cut_qkv")
    up_columns = [[(j * ff_own, 0, ff_own)] for j in range(n_shard)]
    attn_all, up_later = tie((attn_all, up_weight))
    up_weights = reshard(up_later, up_columns, ff_own, "cut_up")
    edge = depth
    to_next = [(i, i + 1) for i in range(n_shard - 1)]
    to_last = [(i + 1, i) for i in range(n_shard - 1)]
    out_long = jnp.concatenate(
        [
            lax.ppermute(out_weight[rows_own - edge :], "shard", to_next),
            out_weight,
            lax.ppermute(out_weight[:edge], "shard", to_last),
        ],
        axis=0,
    )
    out_here = lax.dynamic_slice_in_dim(out_long, edge - own_offset, width, 0)

    grad_low = cotangent.astype(bf16)

    bias_row = jnp.concatenate([bias_query, jnp.zeros((width,), f32), bias_value])[None]
    qkv_here, qkv_all, attended, attended_own, log_totals, middle_part = call(
        partial(attend_kernel, n_shard, window, depth),
        10,
        [
            ((model_width, 3 * width), bf16),
            ((length, 3 * width), bf16),
            ((length, width), bf16),
            ((length, width), bf16),
            ((length, window), f32),
            ((length, model_width), bf16),
        ],
        "attend",
    )(at, *mask_args, attn_all, *qkv_weights, bias_row, out_here)

    middle = hidden_in + scatter_sum(middle_part) + bias_out
    normed_two, inverse_two = normalize(middle)
    ffn_in = (normed_two * gain_two + bias_two).astype(bf16)
    ffn_all = gather(ffn_in)
    grad_all = gather(grad_low)
    act_low, grad_pre_low, ffn_part, pre_sums = call(
        partial(feed_kernel, n_shard),
        7,
        [
            ((length, ff_own), bf16),
            ((length, ff_own), bf16),
            ((length, model_width), bf16),
            ((1, ff_own), f32),
        ],
        "feed",
        [pltpu.VMEM((model_width, ff_own), bf16)],
    )(at, ffn_all, *up_weights, bias_up[None], down_weight, grad_all)

    down_mine = core_rows(product_left(act_low, grad_all))
    down_one, down_two = jnp.split(down_mine, 2)
    down_first = line_sum(down_one)
    grad_ffn_in = scatter_sum(ffn_part)
    grad_ffn_in, down_two = tie((grad_ffn_in, down_two))

    up_mine = core_columns(product_left(ffn_all, grad_pre_low))
    grad_middle = cotangent + norm_back(grad_ffn_in, normed_two, inverse_two, gain_two)
    middle_all = gather(grad_middle.astype(bf16))
    middle_all, up_mine = tie((middle_all, up_mine))
    up_got = to_owners(up_mine)
    pairs = n_shard // 2

    down_two, down_first[0] = tie((down_two, down_first[0]))
    down_second = line_sum(down_two)

    grad_attended = product_right(middle_all, out_here).astype(bf16)
    out_term = lax.dynamic_slice_in_dim(
        product_left(attended_own, middle_all), own_offset, rows_own, 0
    )
    out_mine = core_rows(out_term)

    grad_projected, head_sums = call(
        partial(attend_back_kernel, window, depth),
        8,
        [((length, 3 * width), bf16), ((1, 3 * width), f32)],
        "attend_back",
    )(at, *mask_args, qkv_all, attended, grad_attended, log_totals)

    qkv_mine = core_columns(product_left(attn_all, grad_projected))
    qkv_got = to_owners(qkv_mine)
    grad_later, qkv_mine = tie((grad_projected, qkv_mine))
    grad_attn_in = scatter_sum(product_right(grad_later, qkv_here))

    up_one, down_second[0] = tie((jnp.concatenate(up_got[:pairs]), down_second[0]))
    up_first = line_sum(up_one)
    up_two, up_first[0] = tie((jnp.concatenate(up_got[pairs:]), up_first[0]))
    up_second = line_sum(up_two)
    out_mine, up_second[0] = tie((out_mine, up_second[0]))
    out_piece = line_sum(out_mine)
    qkv_one, out_piece[0] = tie((jnp.concatenate(qkv_got[:pairs]), out_piece[0]))
    qkv_first = line_sum(qkv_one)
    qkv_two, qkv_first[0] = tie((jnp.concatenate(qkv_got[pairs:]), qkv_first[0]))
    qkv_second = line_sum(qkv_two)

    input_grad = grad_middle + norm_back(grad_attn_in, normed_one, inverse_one, gain_one)
    block_out = middle + scatter_sum(product(act_low, down_weight)) + bias_down

    def finish(first, second, shape, columns, total, name):
        ends = [first[-1], second[-1]] if second else [first[-1]]
        others = [partner(end) for end in ends]
        pieces = jnp.concatenate(ends).reshape(shape)
        return place(pieces, jnp.concatenate(others).reshape(shape), columns, total, name)

    half = rows_own // 2
    whole_row = [[(0, 0, model_width)]]
    down_grad = finish(
        down_first, down_second, (1, ff_own // 2, model_width), whole_row, model_width, "place_down"
    )
    up_grad = finish(
        up_first,
        up_second,
        (n_shard, half, ff_own),
        [[(0, j * ff_own, ff_own)] for j in range(n_shard)],
        n_shard * ff_own,
        "place_up",
    )
    out_grad = finish(
        out_piece, None, (1, half, model_width), whole_row, model_width, "place_out"
    )
    qkv_grad = finish(
        qkv_first,
        qkv_second,
        (n_shard, half, 3 * width),
        [
            [(p * width + offsets[j], p * model_width + j * rows_own, rows_own) for p in range(3)]
            for j in range(n_shard)
        ],
        3 * model_width,
        "place_qkv",
    )

    head_first = jnp.asarray([s * depth for s in starts], jnp.int32)[me]
    blank = jnp.zeros((1, model_width), f32)
    query_sums = lax.dynamic_update_slice(blank, head_sums[:, :width], (0, head_first))
    value_sums = lax.dynamic_update_slice(blank, head_sums[:, 2 * width :], (0, head_first))
    pre_sums = lax.dynamic_update_slice(
        jnp.zeros((n_shard, ff_own), f32), pre_sums, (me, 0)
    ).reshape(4, model_width)
    vector_terms = jnp.concatenate(
        [
            jnp.stack(
                [jnp.sum(grad_attn_in * normed_one, axis=0), jnp.sum(grad_attn_in, axis=0)]
            ),
            query_sums,
            value_sums,
            jnp.stack(
                [
                    jnp.sum(grad_middle, axis=0),
                    jnp.sum(grad_ffn_in * normed_two, axis=0),
                    jnp.sum(grad_ffn_in, axis=0),
                    jnp.sum(cotangent, axis=0),
                ]
            ),
            pre_sums,
        ],
        axis=0,
    )
    vector_cut = vector_terms.reshape(12, n_shard, rows_own).transpose(1, 0, 2)
    vector_grad = sum(swap([pick(vector_cut, me ^ d) for d in range(n_shard)]))
    step = 1
    while step < n_rep:
        vector_grad = vector_grad + lax.ppermute(
            vector_grad, "rep", [(i, i ^ step) for i in range(n_rep)]
        )
        step *= 2
    return (block_out, input_grad, qkv_grad, out_grad, up_grad, down_grad, vector_grad)


def solution(mesh):
    placed = (
        P(("rep", "shard"), None),
        P("rep", None),
        P("rep", None),
        P("shard", None),
        P("shard", None),
        P("shard", None),
        P("shard", None),
        P(None, "shard"),
        P(("rep", "shard"), None),
    )
    return jax.shard_map(
        partial(on_device, (mesh.shape["rep"], mesh.shape["shard"])),
        mesh=mesh,
        in_specs=placed,
        out_specs=(
            P(("rep", "shard"), None),
            P(("rep", "shard"), None),
            P("shard", None),
            P("shard", None),
            P("shard", None),
            P("shard", None),
            P(None, "shard"),
        ),
        check_vma=False,
    )
```

```python
from functools import partial
import math

import jax
import jax.numpy as jnp
from jax import lax
from jax.experimental import pallas as pl
from jax.experimental.pallas import tpu as pltpu
from jax.sharding import PartitionSpec as P

HEADS = 25


eps_norm = 1e-05
gelu_c = math.sqrt(2.0 / math.pi)
f32 = jnp.float32
bf16 = jnp.bfloat16


def product(left_side, right_side):
    return jnp.dot(left_side, right_side, preferred_element_type=f32)


def product_left(left_side, right_side):
    return lax.dot_general(
        left_side, right_side, (((0,), (0,)), ((), ())), preferred_element_type=f32
    )


def product_right(left_side, right_side):
    return lax.dot_general(
        left_side, right_side, (((1,), (1,)), ((), ())), preferred_element_type=f32
    )


def normalize(inputs):
    average = jnp.mean(inputs, axis=1, keepdims=True)
    centred = inputs - average
    inverse = lax.rsqrt(jnp.mean(centred * centred, axis=1, keepdims=True) + eps_norm)
    return (centred * inverse, inverse)


def norm_back(upstream, normed, inverse, gain_row):
    scaled = upstream * gain_row
    return inverse * (
        scaled
        - jnp.mean(scaled, axis=1, keepdims=True)
        - normed * jnp.mean(scaled * normed, axis=1, keepdims=True)
    )


def gelu_pair(preact):
    tangent = jnp.tanh(gelu_c * (preact + 0.044715 * preact * preact * preact))
    activated = 0.5 * preact * (1.0 + tangent)
    derivative = 0.5 * (1.0 + tangent) + 0.5 * preact * (1.0 - tangent * tangent) * gelu_c * (
        1.0 + 0.134145 * preact * preact
    )
    return (activated, derivative)


def allowed_pairs(pos_col, pos_row, seg_col, seg_row):
    return (pos_row[...] <= pos_col[...]) & (seg_row[...] == seg_col[...])


def cut_kernel(n_shard, columns, at_ref, w_ref, sent_ref, own_ref):
    me, core = at_ref[0], at_ref[1]
    rows = w_ref.shape[0]
    half = rows // 2

    def one(d, carry):
        for j in range(n_shard):
            for c in range(2):

                @pl.when((me ^ d == j) & (core == c))
                def _():
                    for start, to, size in columns[j]:
                        sent_ref[d - 1, :, to : to + size] = w_ref[
                            c * half : (c + 1) * half, start : start + size
                        ]

        return carry

    lax.fori_loop(1, n_shard, one, 0)
    for j in range(n_shard):

        @pl.when(me == j)
        def _():
            for start, to, size in columns[j]:
                own_ref[:, to : to + size] = w_ref[:, start : start + size]


def place_kernel(n_places, columns, *refs):
    at_ref, out_ref = refs[0], refs[-1]
    pieces = (len(refs) - 2) // 2
    mine_refs, other_refs = refs[1 : 1 + pieces], refs[1 + pieces : -1]
    me, core = at_ref[0], at_ref[1]
    half = out_ref.shape[0] // 2
    rows = half * n_places // pieces
    for piece in range(pieces):
        for part in range(max(1, n_places // pieces)):
            d = piece * n_places // pieces + part
            size = min(rows, half)
            first = (piece * rows) % half
            local = part * half if n_places >= pieces else 0
            for j in range(n_places):
                for c in range(2):

                    @pl.when(((me ^ d == j) | (n_places == 1)) & (core == c))
                    def _():
                        for start, to, wide in columns[j]:
                            for side, ref in ((c, mine_refs[piece]), (1 - c, other_refs[piece])):
                                top = side * half + first
                                out_ref[top : top + size, to : to + wide] = ref[
                                    local : local + size, start : start + wide
                                ].astype(f32)


def assemble(n_shard, at_ref, own_ref, mine_refs, other_refs, full_ref):
    me, core = at_ref[0], at_ref[1]
    rows = own_ref.shape[0]
    half = rows // 2
    for j in range(n_shard):
        first = j * rows

        @pl.when(me == j)
        def _():
            full_ref[first : first + rows, :] = own_ref[...]

        for d in range(1, n_shard):
            for c in range(2):

                @pl.when((me ^ d == j) & (core == c))
                def _():
                    low, high = (mine_refs, other_refs) if c == 0 else (other_refs, mine_refs)
                    full_ref[first : first + half, :] = low[d - 1][...]
                    full_ref[first + half : first + rows, :] = high[d - 1][...]


def join_rows(refs, full_ref):
    rows = refs[0].shape[0]
    for d, ref in enumerate(refs):
        full_ref[d * rows : (d + 1) * rows, :] = ref[...]


def term_kernel(groups, at_ref, left_ref, right_ref, sent_ref, kept_ref, full_ref):
    full_ref[...] = product_left(left_ref[...], right_ref[...]).astype(bf16)
    half = full_ref.shape[0] // (2 * groups)
    for c in range(2):

        @pl.when(at_ref[1] == c)
        def _():
            for g in range(groups):
                first = 2 * g * half
                kept_ref[g] = full_ref[first + c * half : first + (c + 1) * half, :]
                sent_ref[g] = full_ref[first + (1 - c) * half : first + (2 - c) * half, :]


def attend_kernel(n_shard, window, depth, *refs):
    at_ref, pos_col, pos_row, seg_col, seg_row, bias_ref, out_w, own_w = refs[:8]
    refs = refs[8:]
    others = n_shard - 1
    mine_w, other_w, h_parts = refs[:others], refs[others : 2 * others], refs[2 * others : 3 * others + 1]
    w_ref, h_ref, qkv_ref, o_ref, own_o_ref, lse_ref, part_ref = refs[3 * others + 1 :]
    join_rows(h_parts, h_ref)
    assemble(n_shard, at_ref, own_w, mine_w, other_w, w_ref)
    qkv_ref[...] = (product(h_ref[...], w_ref[...]) + bias_ref[...]).astype(bf16)
    allowed = allowed_pairs(pos_col, pos_row, seg_col, seg_row)
    factor = 1.0 / math.sqrt(depth)
    width = window * depth
    for head in range(window):
        q_at, k_at, v_at = (
            slice(p * width + head * depth, p * width + (head + 1) * depth) for p in range(3)
        )
        scores = product_right(qkv_ref[:, q_at], qkv_ref[:, k_at]) * factor
        masked = jnp.where(allowed, scores, -1e30)
        highest = jnp.max(masked, axis=1, keepdims=True)
        raised = jnp.exp(masked - highest)
        total = jnp.sum(raised, axis=1, keepdims=True)
        weights = (raised * (1.0 / total)).astype(bf16)
        attended = product(weights, qkv_ref[:, v_at])
        o_ref[:, q_at] = attended.astype(bf16)
        lse_ref[:, head : head + 1] = highest + jnp.log(total)
    first = at_ref[2]
    column = lax.broadcasted_iota(jnp.int32, o_ref.shape, 1)
    inside = (column >= first) & (column < first + at_ref[3])
    own_o_ref[...] = jnp.where(inside, o_ref[...].astype(f32), 0.0).astype(bf16)
    store_parts(product(own_o_ref[...], out_w[...]), part_ref)


def store_parts(total, part_ref):
    part_ref[...] = total.astype(bf16).reshape(part_ref.shape)


def feed_kernel(n_shard, *refs):
    at_ref, bias_ref, down_ref, own_w = refs[:4]
    refs = refs[4:]
    others = n_shard - 1
    mine_w, other_w = refs[:others], refs[others : 2 * others]
    h_parts, y_parts = refs[2 * others : 3 * others + 1], refs[3 * others + 1 : 4 * others + 2]
    h_ref, y_ref, act_ref, low_ref, part_ref, sums_ref, w_ref = refs[4 * others + 2 :]
    join_rows(h_parts, h_ref)
    join_rows(y_parts, y_ref)
    assemble(n_shard, at_ref, own_w, mine_w, other_w, w_ref)
    activated, derivative = gelu_pair(product(h_ref[...], w_ref[...]) + bias_ref[...])
    act_ref[...] = activated.astype(bf16)
    grad_pre = product_right(y_ref[...], down_ref[...]) * derivative
    sums_ref[...] = jnp.sum(grad_pre, axis=0, keepdims=True)
    low_ref[...] = grad_pre.astype(bf16)
    store_parts(product_right(low_ref[...], w_ref[...]), part_ref)


def attend_back_kernel(
    window,
    depth,
    at_ref,
    pos_col,
    pos_row,
    seg_col,
    seg_row,
    qkv_ref,
    o_ref,
    go_ref,
    lse_ref,
    gp_ref,
    sums_ref,
):
    allowed = allowed_pairs(pos_col, pos_row, seg_col, seg_row)
    factor = 1.0 / math.sqrt(depth)
    width = window * depth
    first = at_ref[2]
    last = first + at_ref[3]
    for head in range(window):
        columns = slice(head * depth, (head + 1) * depth)
        queries, keys, values = (
            qkv_ref[:, p * width + head * depth : p * width + (head + 1) * depth]
            for p in range(3)
        )
        grad_head = go_ref[:, columns]
        scores = product_right(queries, keys) * factor
        weights = jnp.where(allowed, jnp.exp(scores - lse_ref[:, head : head + 1]), 0.0)
        row_dot = jnp.sum(
            grad_head.astype(f32) * o_ref[:, columns].astype(f32), axis=1, keepdims=True
        )
        grad_weights = product_right(grad_head, values)
        grad_scores = (weights * (grad_weights - row_dot)).astype(bf16)
        grad_query = product(grad_scores, keys) * factor
        grad_keys = product_left(grad_scores, queries) * factor
        grad_values = product_left(weights.astype(bf16), grad_head)
        column = lax.broadcasted_iota(jnp.int32, (1, depth), 1) + head * depth
        inside = (column >= first) & (column < last)
        for place, grad in enumerate((grad_query, grad_keys, grad_values)):
            own = jnp.where(inside, grad, 0.0)
            where_to = slice(place * width + head * depth, place * width + (head + 1) * depth)
            gp_ref[:, where_to] = own.astype(bf16)
            sums_ref[:, where_to] = jnp.sum(own, axis=0, keepdims=True)


def on_device(
    sizes,
    hidden_in,
    segment_ids,
    span_order,
    qkv_weight,
    out_weight,
    up_weight,
    down_weight,
    vectors,
    cotangent,
):
    n_rep, n_shard = sizes
    tokens_here, model_width = hidden_in.shape
    depth = model_width // HEADS
    rows_own = model_width // n_shard
    ff_own = down_weight.shape[0]
    length = tokens_here * n_shard
    me = lax.axis_index("shard")
    rep = lax.axis_index("rep")
    core = rep % 2
    line = rep // 2
    n_line = n_rep // 2

    windows = [
        (i * rows_own // depth, -(-(i + 1) * rows_own // depth)) for i in range(n_shard)
    ]
    window = max(stop - start for start, stop in windows)
    starts = [min(start, HEADS - window) for start, _ in windows]
    width = window * depth
    offsets = [i * rows_own - starts[i] * depth for i in range(n_shard)]
    own_offset = jnp.asarray(offsets, jnp.int32)[me]

    tie = lax.optimization_barrier

    def xor(d):
        return [(i, i ^ d) for i in range(n_shard)]

    def swap(parts):
        return [parts[0]] + [
            lax.ppermute(parts[d], "shard", xor(d)) for d in range(1, n_shard)
        ]

    def gather(part):
        return swap([part] * n_shard)

    def scatter_sum(pieces):
        got = swap([pieces[d] for d in range(n_shard)])
        return sum(piece.astype(f32) for piece in got[1:]) + got[0].astype(f32)

    def pick(stacked, index):
        return lax.dynamic_index_in_dim(stacked, index, 0, keepdims=False)

    def partner(part):
        return lax.ppermute(part, "rep", [(i, i ^ 1) for i in range(n_rep)])

    def by_place(parts):
        stacked = jnp.stack(parts)
        return [pick(stacked, me ^ j) for j in range(n_shard)]

    vmem = pl.BlockSpec(memory_space=pltpu.VMEM)
    smem = pl.BlockSpec(memory_space=pltpu.SMEM)
    params = pltpu.CompilerParams(vmem_limit_bytes=60 * 1024 * 1024)
    at = jnp.stack([me, core, own_offset, jnp.int32(rows_own)]).astype(jnp.int32)

    def call(body, args, shapes, name, scratch=()):
        return pl.pallas_call(
            body,
            in_specs=[smem] + [vmem] * len(args),
            out_specs=[vmem] * len(shapes),
            out_shape=[jax.ShapeDtypeStruct(*shape) for shape in shapes],
            scratch_shapes=scratch,
            compiler_params=params,
            name=name,
        )(at, *args)

    half = rows_own // 2

    def cut(weight, columns, size, name):
        sent, own = call(
            partial(cut_kernel, n_shard, columns),
            [weight],
            [((n_shard - 1, half, size), bf16), ((rows_own, size), bf16)],
            name,
        )
        return sent, own

    def reshard(sent, own):
        mine = swap([None] + [sent[d] for d in range(n_shard - 1)])[1:]
        return [own] + mine + [partner(piece) for piece in mine]

    def core_term(left, right, groups, name):
        shape = ((groups, left.shape[1] // (2 * groups), right.shape[1]), bf16)
        sent, kept = call(
            partial(term_kernel, groups),
            [left, right],
            [shape, shape],
            name,
            [pltpu.VMEM((left.shape[1], right.shape[1]), bf16)],
        )
        return (kept.astype(f32) + partner(sent).astype(f32)).astype(bf16)

    def hop(part, hops):
        return lax.ppermute(
            part, "rep", [(2 * a + c, 2 * b + c) for a, b in hops for c in range(2)]
        )

    inner = n_line // 2

    def line_in(part, got=None):
        return hop(part, [(0, 1), (n_line - 1, n_line - 2)])

    def line_middle(part, got):
        for s in range(inner - 1):
            part = (part.astype(f32) + got.astype(f32)).astype(bf16)
            if s < inner - 2:
                got = hop(part, [(s + 1, s + 2), (n_line - 2 - s, n_line - 3 - s)])
        got = hop(part, [(inner - 1, inner), (inner, inner - 1)])
        return part, got

    def line_out(part, got):
        total = (part.astype(f32) + got.astype(f32)).astype(bf16)
        for s in reversed(range(inner - 1)):
            got = hop(total, [(s + 1, s), (n_line - 2 - s, n_line - 1 - s)])
            outside = (line <= s) | (line >= n_line - 1 - s)
            total = jnp.where(outside, got, total)
        return total

    def to_owners(mine):
        return swap([pick(mine, me ^ d) for d in range(n_shard)])

    vector_parts = swap([vectors] * n_shard)
    vector_wide = jnp.concatenate(by_place(vector_parts), axis=1).astype(f32)
    gain_one = vector_wide[0]
    bias_one = vector_wide[1]
    bias_out = vector_wide[4]
    gain_two = vector_wide[5]
    bias_two = vector_wide[6]
    bias_down = vector_wide[7]
    bias_up = pick(vector_wide[8:12].reshape(n_shard, ff_own), me)
    spans = jnp.stack(
        [
            vector_wide[2:4, start * depth : start * depth + width]
            for start in starts
        ]
    )
    bias_query, bias_value = pick(spans, me)

    order_row = span_order[0]
    within = jnp.arange(tokens_here, dtype=jnp.int32)
    firsts = [order_row[me ^ d] * tokens_here for d in range(n_shard)]
    pos = jnp.concatenate([first + within for first in firsts])
    seg = jnp.concatenate(
        [lax.dynamic_slice(segment_ids[0], (first,), (tokens_here,)) for first in firsts]
    )
    mask_args = (pos[:, None], pos[None, :], seg[:, None], seg[None, :])

    normed_one, inverse_one = normalize(hidden_in)
    attn_in = (normed_one * gain_one + bias_one).astype(bf16)
    qkv_columns = [
        [(p * model_width + starts[j] * depth, p * width, width) for p in range(3)]
        for j in range(n_shard)
    ]
    qkv_weights = reshard(*cut(qkv_weight, qkv_columns, 3 * width, "cut_qkv"))
    attn_parts = gather(attn_in)
    up_columns = [[(j * ff_own, 0, ff_own)] for j in range(n_shard)]
    up_sent, up_own = cut(up_weight, up_columns, ff_own, "cut_up")
    attn_parts[-1], up_sent, out_later = tie((attn_parts[-1], up_sent, out_weight))
    edge = depth
    to_next = [(i, i + 1) for i in range(n_shard - 1)]
    to_last = [(i + 1, i) for i in range(n_shard - 1)]
    out_long = jnp.concatenate(
        [
            lax.ppermute(out_later[rows_own - edge :], "shard", to_next),
            out_later,
            lax.ppermute(out_later[:edge], "shard", to_last),
        ],
        axis=0,
    )
    out_here = lax.dynamic_slice_in_dim(out_long, edge - own_offset, width, 0)
    up_weights = reshard(up_sent, up_own)

    grad_low = cotangent.astype(bf16)

    bias_row = jnp.concatenate([bias_query, jnp.zeros((width,), f32), bias_value])[None]
    parts_shape = ((n_shard, tokens_here, model_width), bf16)
    qkv_here, attn_all, qkv_all, attended, attended_own, log_totals, middle_part = call(
        partial(attend_kernel, n_shard, window, depth),
        [*mask_args, bias_row, out_here, *qkv_weights, *attn_parts],
        [
            ((model_width, 3 * width), bf16),
            ((length, model_width), bf16),
            ((length, 3 * width), bf16),
            ((length, width), bf16),
            ((length, width), bf16),
            ((length, window), f32),
            parts_shape,
        ],
        "attend",
    )

    middle = hidden_in + scatter_sum(middle_part) + bias_out
    normed_two, inverse_two = normalize(middle)
    ffn_in = (normed_two * gain_two + bias_two).astype(bf16)
    ffn_parts = gather(ffn_in)
    grad_parts = gather(grad_low)
    ffn_all, grad_all, act_low, grad_pre_low, ffn_part, pre_sums = call(
        partial(feed_kernel, n_shard),
        [bias_up[None], down_weight, *up_weights, *ffn_parts, *grad_parts],
        [
            ((length, model_width), bf16),
            ((length, model_width), bf16),
            ((length, ff_own), bf16),
            ((length, ff_own), bf16),
            parts_shape,
            ((1, ff_own), f32),
        ],
        "feed",
        [pltpu.VMEM((model_width, ff_own), bf16)],
    )

    down_mine = core_term(act_low, grad_all, 1, "term_down")[0]
    down_one, down_two = jnp.split(down_mine, 2)
    down_one_in, down_two_in = line_in(down_one), line_in(down_two)
    grad_ffn_in = scatter_sum(ffn_part)
    up_mine = core_term(ffn_all, grad_pre_low, n_shard, "term_up")
    grad_ffn_in, down_one = tie((grad_ffn_in, down_one))
    grad_middle = cotangent + norm_back(grad_ffn_in, normed_two, inverse_two, gain_two)
    middle_parts = gather(grad_middle.astype(bf16))
    middle_all = jnp.concatenate(middle_parts, axis=0)
    middle_all, up_mine, down_one_in = tie((middle_all, up_mine, down_one_in))
    up_got = to_owners(up_mine)
    pairs = n_shard // 2
    down_one = line_middle(down_one, down_one_in)

    grad_attended = product_right(middle_all, out_here).astype(bf16)
    out_term = lax.dynamic_slice_in_dim(
        product_left(attended_own, middle_all), own_offset, rows_own, 0
    ).astype(bf16)
    out_term = out_term.reshape(2, half, model_width)

    grad_projected, head_sums = call(
        partial(attend_back_kernel, window, depth),
        [*mask_args, qkv_all, attended, grad_attended, log_totals],
        [((length, 3 * width), bf16), ((1, 3 * width), f32)],
        "attend_back",
    )

    grad_projected, down_two_in = tie((grad_projected, down_two_in))
    down_two = line_middle(down_two, down_two_in)
    up_one, down_two_in = tie((jnp.concatenate(up_got[:pairs]), down_two_in))
    up_two = jnp.concatenate(up_got[pairs:])
    up_one_in = line_in(up_one)

    qkv_mine = core_term(attn_all, grad_projected, n_shard, "term_qkv")
    qkv_got = to_owners(qkv_mine)
    grad_later, qkv_mine = tie((grad_projected, qkv_mine))
    e1_part = product_right(grad_later, qkv_here).astype(bf16)
    grad_attn_in = scatter_sum(e1_part.reshape(n_shard, tokens_here, model_width))
    out_mine = (
        pick(out_term, core).astype(f32) + partner(pick(out_term, 1 - core)).astype(f32)
    ).astype(bf16)

    up_one_in, up_two = tie((up_one_in, up_two))
    up_two_in = line_in(up_two)
    up_one = line_middle(up_one, up_one_in)
    up_two_in, out_mine = tie((up_two_in, out_mine))
    out_in = line_in(out_mine)
    up_two = line_middle(up_two, up_two_in)
    qkv_one, out_in = tie((jnp.concatenate(qkv_got[:pairs]), out_in))
    qkv_one_in = line_in(qkv_one)
    out_mid = line_middle(out_mine, out_in)
    qkv_two, qkv_one_in = tie((jnp.concatenate(qkv_got[pairs:]), qkv_one_in))
    qkv_two_in = line_in(qkv_two)
    qkv_one = line_middle(qkv_one, qkv_one_in)
    qkv_two = line_middle(qkv_two, qkv_two_in)

    input_grad = grad_middle + norm_back(grad_attn_in, normed_one, inverse_one, gain_one)
    block_part = product(act_low, down_weight).astype(bf16)
    block_out = (
        middle + scatter_sum(block_part.reshape(n_shard, tokens_here, model_width)) + bias_down
    )

    def place(totals, columns, total, name):
        others = [partner(piece) for piece in totals]
        rows = 2 * sum(piece.shape[0] for piece in totals) // len(columns)
        return call(
            partial(place_kernel, len(columns), columns),
            [*totals, *others],
            [((rows, total), f32)],
            name,
        )[0]

    whole_row = [[(0, 0, model_width)]]
    down_grad = place(
        [line_out(*down_one), line_out(*down_two)], whole_row, model_width, "place_down"
    )
    qkv_one = (qkv_one[0], tie((qkv_one[1], down_grad)))
    down_grad = qkv_one[1][1]
    qkv_one = line_out(qkv_one[0], qkv_one[1][0])
    up_grad = place(
        [line_out(*up_one), line_out(*up_two)],
        [[(0, j * ff_own, ff_own)] for j in range(n_shard)],
        n_shard * ff_own,
        "place_up",
    )
    out_grad = place([line_out(*out_mid)], whole_row, model_width, "place_out")
    qkv_two_got, up_grad, out_grad = tie((qkv_two[1], up_grad, out_grad))
    qkv_two = line_out(qkv_two[0], qkv_two_got)
    qkv_grad = place(
        [qkv_one, qkv_two],
        [
            [(p * width + offsets[j], p * model_width + j * rows_own, rows_own) for p in range(3)]
            for j in range(n_shard)
        ],
        3 * model_width,
        "place_qkv",
    )

    head_first = jnp.asarray([s * depth for s in starts], jnp.int32)[me]
    blank = jnp.zeros((1, model_width), f32)
    query_sums = lax.dynamic_update_slice(blank, head_sums[:, :width], (0, head_first))
    value_sums = lax.dynamic_update_slice(blank, head_sums[:, 2 * width :], (0, head_first))
    pre_sums = lax.dynamic_update_slice(
        jnp.zeros((n_shard, ff_own), f32), pre_sums, (me, 0)
    ).reshape(4, model_width)
    vector_terms = jnp.concatenate(
        [
            jnp.stack(
                [jnp.sum(grad_attn_in * normed_one, axis=0), jnp.sum(grad_attn_in, axis=0)]
            ),
            query_sums,
            value_sums,
            jnp.stack(
                [
                    jnp.sum(grad_middle, axis=0),
                    jnp.sum(grad_ffn_in * normed_two, axis=0),
                    jnp.sum(grad_ffn_in, axis=0),
                    jnp.sum(cotangent, axis=0),
                ]
            ),
            pre_sums,
        ],
        axis=0,
    )
    vector_cut = vector_terms.reshape(12, n_shard, rows_own).transpose(1, 0, 2)
    vector_grad = sum(swap([pick(vector_cut, me ^ d) for d in range(n_shard)]))
    step = 1
    while step < n_rep:
        vector_grad = vector_grad + lax.ppermute(
            vector_grad, "rep", [(i, i ^ step) for i in range(n_rep)]
        )
        step *= 2
    return (block_out, input_grad, qkv_grad, out_grad, up_grad, down_grad, vector_grad)


def solution(mesh):
    placed = (
        P(("rep", "shard"), None),
        P("rep", None),
        P("rep", None),
        P("shard", None),
        P("shard", None),
        P("shard", None),
        P("shard", None),
        P(None, "shard"),
        P(("rep", "shard"), None),
    )
    return jax.shard_map(
        partial(on_device, (mesh.shape["rep"], mesh.shape["shard"])),
        mesh=mesh,
        in_specs=placed,
        out_specs=(
            P(("rep", "shard"), None),
            P(("rep", "shard"), None),
            P("shard", None),
            P("shard", None),
            P("shard", None),
            P("shard", None),
            P(None, "shard"),
        ),
        check_vma=False,
    )
```
